512 devices in a mesh: row: 16 (over x, y), col: 32 (over z, core).
Axes of the slice: x: 4, y: 4, z: 16, core: 2. Of those that a mesh axis runs over, the one named last changes fastest.
Arguments:
- front: bfloat16 [16384, 16384], P('row', 'col'), may hold values from -0.046875 to 0.046875
- diag_inverse: float32 [128, 128, 128], P('row'), may hold values from -0.25 to 1.5
- load: float32 [8, 16384], P(None, 'row'), may hold values from -6 to 6
- panel_order: int32 [128], replicated, may hold values from 0 to 127, each once
- tie: float32 [32, 16384], P('col', 'row'), may hold values from 0.5 to 1.5
- mass: float32 [32, 16384], P('col', 'row'), may hold values from 0.5 to 6
- modes: bfloat16 [1024, 32, 16384], P(None, 'col', 'row'), may hold values from -0.0234375 to 0.0234375
Outputs:
- front_solution: float32 [8, 16384], P(None, 'row')
- residual_vectors: float32 [8, 32, 16384], P(None, 'col', 'row')
The draws below stay inside these ranges and needn't reach their ends.
All inputs are finite; a program needn't handle non-finite values.
Results may differ from the reference program's by a relative error of at most 0.0049.
Values may be sent and summed in bfloat16 or wider, within the bound.
No kernel may reach another device: no remote copies, remote signals or barrier semaphores. Data moves between devices by JAX's collectives and lax.ppermute only.
A program may use at most 64 MiB of HBM per device.

```python
import math
import jax
import jax.numpy as jnp
from jax import lax

N = 16384
B = 128
M = 1024
LEVELS = 4
RV = 8
NB = 128
A = 32


def draw_diag_inverse(key, part):
    key_scale, key_jitter = jax.random.split(key)
    factors = jax.random.uniform(key_scale, (NB, B, 1), jnp.float32, 0.8, 1.25)
    jitter = jnp.clip(jax.random.normal(key_jitter, (NB, B, B), jnp.float32) * (0.5 / math.sqrt(B)), -0.25, 0.25)
    return jnp.eye(B, dtype=jnp.float32)[None, :, :] * factors + jitter


def draw_mass(key, part):
    rise_copy = 1.0 + jnp.arange(A, dtype=jnp.float32)[:, None] / A
    rise_front = 1.0 + jnp.arange(N, dtype=jnp.float32)[None, :] / N
    rough = jax.random.uniform(key, (A, N), jnp.float32, 0.5, 1.5)
    return rise_copy * rise_front * rough


def block_scale(own_key, dims, pieces, least, top_value):
    level = 1.0
    for position, blocks in pieces:
        draws = jax.random.uniform(jax.random.fold_in(jax.random.fold_in(own_key, 6), position), (blocks,), jnp.float32, least / len(pieces), top_value / len(pieces))
        level = level * jnp.repeat(jnp.exp(draws), dims[position] // blocks).reshape((-1,) + (1,) * (len(dims) - 1 - position))
    return level


def centred(own_key, dims, scale, limit, shards=(), kind=jnp.bfloat16):
    array = scale * jax.random.normal(own_key, dims, jnp.float32)
    if shards:
        array = array * block_scale(own_key, dims, shards, -0.22, 0.18)
    return jnp.clip(array, -limit, limit).astype(kind)


def setup_inputs(seed: int = 0) -> dict:
    splits = jax.random.split(jax.random.key(seed), 8)
    front = centred(splits[0], (N, N), N ** -0.5, 0.046875, ((0, 16), (1, 32)))
    diag_inverse = draw_diag_inverse(jax.random.fold_in(splits[7], 71), 0)
    load = centred(splits[2], (RV, N), 1.0, 6.0, ((1, 16),), jnp.float32)
    panel_order = jax.random.permutation(splits[3], NB).astype(jnp.int32)
    tie = jnp.clip(1.0 + 0.1 * jax.random.normal(splits[4], (A, N), jnp.float32), 0.5, 1.5)
    mass = draw_mass(jax.random.fold_in(splits[7], 71), 0)
    modes = centred(splits[6], (M, A, N), (A * N // 8) ** -0.5, 0.0234375, ((1, 32), (2, 16)))
    return {"front": front, "diag_inverse": diag_inverse, "load": load, "panel_order": panel_order, "tie": tie, "mass": mass, "modes": modes}


highest = lax.Precision.HIGHEST


def reference(front, diag_inverse, load, panel_order, tie, mass, modes):
    panels = N // B
    ranks = jnp.zeros((panels,), jnp.int32).at[panel_order].set(jnp.arange(panels, dtype=jnp.int32))
    levels_of = ranks // (panels // LEVELS)
    position_level = jnp.repeat(levels_of, B)
    pending = jnp.zeros((RV, N), jnp.float32)
    forward_out = jnp.zeros((RV, N), jnp.float32)
    for level in range(LEVELS):
        remain = (load - pending).reshape(RV, panels, B)
        candidate = jnp.einsum("vpj,pij->vpi", remain, diag_inverse, precision=highest).reshape(RV, N)
        chosen = position_level[None, :] == level
        forward_out = jnp.where(chosen, candidate, forward_out)
        fresh = jnp.where(chosen, forward_out, 0.0).astype(jnp.bfloat16)
        pending = pending + jnp.dot(fresh, front.T, preferred_element_type=jnp.float32)
    back_pending = jnp.zeros((RV, N), jnp.float32)
    back_out = jnp.zeros((RV, N), jnp.float32)
    for level in reversed(range(LEVELS)):
        remain = (forward_out - back_pending).reshape(RV, panels, B)
        candidate = jnp.einsum("vpj,pji->vpi", remain, diag_inverse, precision=highest).reshape(RV, N)
        chosen = position_level[None, :] == level
        back_out = jnp.where(chosen, candidate, back_out)
        fresh = jnp.where(chosen, back_out, 0.0).astype(jnp.bfloat16)
        back_pending = back_pending + jnp.dot(fresh, front, preferred_element_type=jnp.float32)
    static = tie[None, :, :] * back_out[:, None, :]
    weighted = (mass[None, :, :] * static).astype(jnp.bfloat16).reshape(RV, A * N)
    mode_rows = modes.reshape(M, A * N)
    coords = lax.dot_general(weighted, mode_rows, (((1,), (1,)), ((), ())), preferred_element_type=jnp.float32)
    correction = jnp.dot(coords.astype(jnp.bfloat16), mode_rows, preferred_element_type=jnp.float32)
    return back_out, static - correction.reshape(RV, A, N)
```

```python
import jax
import jax.numpy as jnp
from jax import lax
from jax.sharding import Mesh, PartitionSpec as P

LEVELS = 4
PLANE = ("x", "y")

highest = lax.Precision.HIGHEST


def spread(value, axes, count):
    return lax.all_to_all(jnp.broadcast_to(value[None], (count,) + value.shape), axes, 0, 0, tiled=True)


def both_cores(value):
    return lax.all_gather(value, "k", axis=0)


def on_device(front, diag_inverse, load, panel_order, tie, mass, modes):
    vectors = load.shape[0]
    block_size = diag_inverse.shape[1]
    local_panels = diag_inverse.shape[0]
    rows_local = front.shape[0]
    half = front.shape[1]
    half_panels = half // block_size
    panels = panel_order.shape[0]
    plane_at = lax.axis_index(PLANE)
    z_at = lax.axis_index("z")
    core_at = lax.axis_index("k")
    plane_size = lax.axis_size(PLANE)
    z_size = lax.axis_size("z")

    first_panel = plane_at * local_panels + core_at * half_panels
    mine_ids = first_panel + jnp.arange(half_panels, dtype=jnp.int32)
    counting = jnp.arange(panels, dtype=jnp.int32)
    ranks = jnp.sum(jnp.where(panel_order[None, :] == mine_ids[:, None], counting[None, :], 0), axis=1)
    level_of = jnp.repeat(ranks // (panels // LEVELS), block_size)[None, :]

    inverse = lax.dynamic_slice_in_dim(diag_inverse, core_at * half_panels, half_panels, 0)
    load_half = lax.dynamic_slice_in_dim(load, core_at * half, half, 1)

    def solve(value, form):
        value = value.reshape(vectors, half_panels, block_size)
        return jnp.einsum(form, value, inverse, precision=highest).reshape(vectors, half)

    def my_half_sum(value):
        pair = both_cores(value)
        total = pair[0] + pair[1]
        return jnp.where(core_at == 0, total[:, :half], total[:, half:])

    def join(value):
        pair = both_cores(value)
        return jnp.concatenate([pair[0], pair[1]], axis=1)

    def total_over(value, axes, count):
        return jnp.sum(spread(value.astype(jnp.bfloat16), axes, count).astype(jnp.float32), axis=0)

    pending = jnp.zeros((vectors, rows_local), jnp.float32)
    forward_out = jnp.zeros((vectors, half), jnp.float32)
    for level in range(LEVELS):
        remain = load_half
        if level > 0:
            remain = load_half - total_over(my_half_sum(pending), "z", z_size)
        chosen = level_of == level
        candidate = solve(remain, "vpj,pij->vpi")
        forward_out = jnp.where(chosen, candidate, forward_out)
        if level < LEVELS - 1:
            fresh = jnp.where(chosen, candidate, 0.0).astype(jnp.bfloat16)
            mine = lax.dynamic_index_in_dim(spread(fresh, PLANE, plane_size), z_at, 0, keepdims=False)
            pending = pending + lax.dot_general(
                mine, front, (((1,), (1,)), ((), ())), preferred_element_type=jnp.float32
            )

    back_pending = jnp.zeros((vectors, half), jnp.float32)
    back_out = jnp.zeros((vectors, half), jnp.float32)
    for level in reversed(range(LEVELS)):
        chosen = level_of == level
        if level == LEVELS - 1:
            solved = jnp.where(chosen, solve(forward_out, "vpj,pji->vpi"), 0.0)
            back_out = solved
            fresh = solved.astype(jnp.bfloat16)
        else:
            here = total_over(back_pending, PLANE, plane_size)
            solved = jnp.where(chosen, solve(forward_out - here, "vpj,pji->vpi"), 0.0).astype(jnp.bfloat16)
            fresh = lax.dynamic_index_in_dim(spread(solved, "z", z_size), plane_at, 0, keepdims=False)
            back_out = back_out + fresh.astype(jnp.float32)
        if level > 0:
            back_pending = back_pending + jnp.dot(join(fresh), front, preferred_element_type=jnp.float32)

    solution_rows = join(back_out)
    static = tie * solution_rows
    weighted = (mass * static).astype(jnp.bfloat16)
    mode_rows = modes.reshape(modes.shape[0], -1)
    coords = lax.dot_general(
        weighted, mode_rows, (((1,), (1,)), ((), ())), preferred_element_type=jnp.float32
    )
    coords = total_over(my_half_sum(coords), PLANE, plane_size)
    coords = total_over(coords, "z", z_size)
    coords = join(coords.astype(jnp.bfloat16))
    correction = jnp.dot(coords, mode_rows, preferred_element_type=jnp.float32)
    return solution_rows, (static - correction)[:, None, :]


def solution(mesh):
    grid = Mesh(mesh.devices.reshape(4, 4, 16, 2), ("x", "y", "z", "k"))
    row, col = PLANE, ("z", "k")
    in_specs = (
        P(row, col),
        P(row, None, None),
        P(None, row),
        P(),
        P(col, row),
        P(col, row),
        P(None, col, row),
    )
    out_specs = (P(None, row), P(None, col, row))
    return jax.shard_map(
        on_device, mesh=grid, in_specs=in_specs, out_specs=out_specs, check_vma=False
    )
```

```python
import jax
import jax.numpy as jnp
from jax import lax
from jax.experimental import pallas as pl
from jax.experimental.pallas import tpu as pltpu
from jax.sharding import Mesh, PartitionSpec as P

LEVELS = 4
PLANE = ("x", "y")
F32, BF16 = jnp.float32, jnp.bfloat16


def matmul(a, b, form):
    dims = {"nn": (((1,), (0,)), ((), ())), "nt": (((1,), (1,)), ((), ()))}[form]
    return lax.dot_general(a, b, dims, preferred_element_type=F32)


def split(value):
    high = value.astype(BF16)
    return high, (value - high.astype(F32)).astype(BF16)


class Far:
    def __init__(self, array):
        self.array = array


def call(body, outs, *args, scratch=()):
    vmem = pl.BlockSpec(memory_space=pltpu.VMEM)
    in_specs, given = [], []
    for arg in args:
        if isinstance(arg, Far):
            in_specs.append(pl.BlockSpec(memory_space=pltpu.HBM))
            given.append(pltpu.with_memory_space_constraint(arg.array, pltpu.HBM))
        else:
            in_specs.append(vmem)
            given.append(pltpu.with_memory_space_constraint(arg, pltpu.VMEM))
    return pl.pallas_call(
        body,
        out_shape=[out if isinstance(out, jax.ShapeDtypeStruct) else pltpu.VMEM(*out) for out in outs],
        in_specs=in_specs,
        out_specs=[vmem] * len(outs),
        scratch_shapes=list(scratch),
        compiler_params=pltpu.CompilerParams(vmem_limit_bytes=8 << 20),
    )(*given)


def send_to_all(out_ref, value):
    value = value.astype(BF16)
    for slot in range(out_ref.shape[0]):
        out_ref[slot] = value


def sum_slots(ref):
    total = ref[0].astype(F32)
    for slot in range(1, ref.shape[0]):
        total = total + ref[slot].astype(F32)
    return total


def solve(value, high_ref, low_ref, form):
    panels, block = high_ref.shape[0], high_ref.shape[1]
    out = []
    for p in range(panels):
        top, rest = split(value[:, p * block : (p + 1) * block])
        out.append(
            matmul(top, high_ref[p], form) + (matmul(rest, high_ref[p], form) + matmul(top, low_ref[p], form))
        )
    return jnp.concatenate(out, axis=1)


def start_kernel(
    order_hbm, load_hbm, inverse_hbm, front_hbm,
    level_ref, high_ref, low_ref, mine_ref, y_ref, send_ref, front_ref,
    order_ref, inverse_ref, sems,
):
    panels, block = high_ref.shape[0], high_ref.shape[1]
    half = panels * block
    core = lax.axis_index("k")
    copies = [
        pltpu.make_async_copy(order_hbm, order_ref, sems.at[0]),
        pltpu.make_async_copy(inverse_hbm.at[pl.ds(core * panels, panels)], inverse_ref, sems.at[1]),
        pltpu.make_async_copy(load_hbm.at[:, pl.ds(pl.multiple_of(core * half, half), half)], mine_ref, sems.at[2]),
        pltpu.make_async_copy(front_hbm, front_ref, sems.at[3]),
    ]
    for copy in copies:
        copy.start()
    copies[0].wait()
    order = order_ref[...]
    counting = lax.broadcasted_iota(jnp.int32, order.shape, 1)
    per_level = order.shape[1] // LEVELS
    first = lax.axis_index(PLANE) * (2 * panels) + core * panels
    levels = []
    for p in range(panels):
        rank = jnp.sum(jnp.where(order == first + p, counting, 0), axis=1, keepdims=True)
        level = jnp.zeros_like(rank)
        for bound in range(1, LEVELS):
            level = level + jnp.where(rank >= bound * per_level, 1, 0)
        levels.append(jnp.broadcast_to(level, (level_ref.shape[0], block)))
    level_row = jnp.concatenate(levels, axis=1)
    level_ref[...] = level_row
    copies[1].wait()
    high, low = split(inverse_ref[...])
    high_ref[...] = high
    low_ref[...] = low
    copies[2].wait()
    y = jnp.where(level_row == 0, solve(mine_ref[...], high_ref, low_ref, "nt"), 0.0)
    y_ref[...] = y
    send_to_all(send_ref, y)
    copies[3].wait()


def update_kernel(front_ref, got_ref, *refs):
    out_ref = refs[-1]
    out = matmul(got_ref[lax.axis_index("z")], front_ref[...], "nt")
    if len(refs) == 2:
        out = refs[0][...] + out
    out_ref[...] = out


def pair_kernel(pair_ref, send_ref):
    half = send_ref.shape[2]
    rows = pair_ref[0] + pair_ref[1]
    send_to_all(send_ref, jnp.where(lax.axis_index("k") == 0, rows[:, :half], rows[:, half:]))


def forward_kernel(level, got_ref, mine_ref, level_ref, high_ref, low_ref, y_in_ref, y_ref, send_ref):
    chosen = level_ref[...] == level
    candidate = solve(mine_ref[...] - sum_slots(got_ref), high_ref, low_ref, "nt")
    y_ref[...] = jnp.where(chosen, candidate, y_in_ref[...])
    send_to_all(send_ref, jnp.where(chosen, candidate, 0.0))


def turn_kernel(
    got_ref, mine_ref, level_ref, high_ref, low_ref, y_in_ref, modes_hbm, y_ref, x_ref, fresh_ref, modes_ref, sem
):
    modes_copy = pltpu.make_async_copy(modes_hbm, modes_ref, sem)
    modes_copy.start()
    chosen = level_ref[...] == LEVELS - 1
    candidate = solve(mine_ref[...] - sum_slots(got_ref), high_ref, low_ref, "nt")
    y = jnp.where(chosen, candidate, y_in_ref[...])
    y_ref[...] = y
    x = jnp.where(chosen, solve(y, high_ref, low_ref, "nn"), 0.0)
    x_ref[...] = x
    fresh_ref[...] = x.astype(BF16)
    modes_copy.wait()


def back_update_kernel(first, last, front_ref, pair_ref, *refs):
    half = pair_ref.shape[2]
    out = matmul(pair_ref[0], front_ref[:half], "nn") + matmul(pair_ref[1], front_ref[half:], "nn")
    if not first:
        out = refs[0][...] + out
    if not last:
        refs[-2][...] = out
    send_to_all(refs[-1], out)


def back_kernel(level, got_ref, level_ref, high_ref, low_ref, y_ref, send_ref):
    x = solve(y_ref[...] - sum_slots(got_ref), high_ref, low_ref, "nn")
    send_to_all(send_ref, jnp.where(level_ref[...] == level, x, 0.0))


def pick_kernel(got_ref, x_in_ref, x_ref, fresh_ref):
    fresh = got_ref[lax.axis_index(PLANE)]
    x_ref[...] = x_in_ref[...] + fresh.astype(F32)
    fresh_ref[...] = fresh


def last_pick_kernel(got_ref, x_in_ref, x_ref):
    x_ref[...] = x_in_ref[...] + got_ref[lax.axis_index(PLANE)].astype(F32)


def coords_kernel(pair_ref, tie_ref, mass_ref, modes_ref, x_ref, static_ref, send_ref):
    x = jnp.concatenate([pair_ref[0], pair_ref[1]], axis=1)
    x_ref[...] = x
    static = tie_ref[...] * x
    static_ref[...] = static
    coords = matmul((mass_ref[...] * static).astype(BF16), modes_ref[...], "nt").astype(BF16)
    cores, half = 2, send_ref.shape[2]
    for slot in range(send_ref.shape[0]):
        part = slot % cores
        send_ref[slot] = coords[:, part * half : (part + 1) * half]


def relay_kernel(got_ref, send_ref):
    send_to_all(send_ref, sum_slots(got_ref))


def gathered_kernel(got_ref, out_ref):
    out_ref[...] = sum_slots(got_ref).astype(BF16)


def finish_kernel(static_ref, pair_ref, modes_ref, x_ref, whole_ref, out_ref):
    half = pair_ref.shape[2]
    correction = matmul(pair_ref[0], modes_ref[:half], "nn") + matmul(pair_ref[1], modes_ref[half:], "nn")
    whole_ref[...] = x_ref[...]
    out_ref[:, 0, :] = static_ref[...] - correction


def bound(body, *settings):
    def kernel(*refs):
        body(*settings, *refs)

    return kernel


def on_device(front, diag_inverse, load, panel_order, tie, mass, modes):
    vectors = load.shape[0]
    block = diag_inverse.shape[1]
    rows, half = front.shape
    half_panels = half // block
    plane = lax.axis_size(PLANE)
    depth = lax.axis_size("z")
    cores = lax.axis_size("k")
    mode_rows = modes.reshape(modes.shape[0], -1)

    small = ((vectors, half), F32)
    narrow = ((vectors, half), BF16)
    to_plane = ((plane, vectors, half), BF16)
    to_depth = ((depth, vectors, half), BF16)
    inverse_half = ((half_panels, block, block), BF16)

    def exchange(value, axes):
        return lax.all_to_all(value, axes, 0, 0, tiled=True)

    def both_cores(value):
        return lax.all_gather(value, "k", axis=0)

    level_row, high, low, mine, y, send, front = call(
        start_kernel,
        [((vectors, half), jnp.int32), inverse_half, inverse_half, small, small, to_plane, (front.shape, BF16)],
        Far(panel_order[None, :]), Far(load), Far(diag_inverse), Far(front),
        scratch=[
            pltpu.VMEM((1, panel_order.shape[0]), jnp.int32),
            pltpu.VMEM((half_panels, block, block), F32),
            pltpu.SemaphoreType.DMA((4,)),
        ],
    )
    pending = ()
    for level in range(1, LEVELS):
        got = exchange(send, PLANE)
        pending = tuple(call(update_kernel, [((vectors, rows), F32)], front, got, *pending))
        (send,) = call(pair_kernel, [to_depth], both_cores(pending[0]))
        got = exchange(send, "z")
        args = (got, mine, level_row, high, low, y)
        if level < LEVELS - 1:
            y, send = call(bound(forward_kernel, level), [small, to_plane], *args)
        else:
            y, x, fresh, mode_rows = call(
                turn_kernel,
                [small, small, narrow, (mode_rows.shape, BF16)],
                *args, Far(mode_rows),
                scratch=[pltpu.SemaphoreType.DMA(())],
            )

    pending = ()
    for level in reversed(range(LEVELS - 1)):
        last = level == 0
        *pending, send = call(
            bound(back_update_kernel, not pending, last),
            [to_plane] if last else [small, to_plane],
            front, both_cores(fresh), *pending,
        )
        got = exchange(send, PLANE)
        (send,) = call(bound(back_kernel, level), [to_depth], got, level_row, high, low, y)
        got = exchange(send, "z")
        if level > 0:
            x, fresh = call(pick_kernel, [small, narrow], got, x)
        else:
            (x,) = call(last_pick_kernel, [small], got, x)

    whole, static, send = call(
        coords_kernel,
        [((vectors, rows), F32), ((vectors, rows), F32), ((plane * cores, vectors, half), BF16)],
        both_cores(x), tie, mass, mode_rows,
    )
    (send,) = call(relay_kernel, [to_depth], exchange(send, PLANE + ("k",)))
    (coords,) = call(gathered_kernel, [narrow], exchange(send, "z"))
    return tuple(
        call(
            finish_kernel,
            [jax.ShapeDtypeStruct((vectors, rows), F32), jax.ShapeDtypeStruct((vectors, 1, rows), F32)],
            static, both_cores(coords), mode_rows, whole,
        )
    )


def solution(mesh):
    grid = Mesh(mesh.devices.reshape(4, 4, 16, 2), PLANE + ("z", "k"))
    row, col = PLANE, ("z", "k")
    in_specs = (
        P(row, col),
        P(row, None, None),
        P(None, row),
        P(),
        P(col, row),
        P(col, row),
        P(None, col, row),
    )
    out_specs = (P(None, row), P(None, col, row))
    return jax.shard_map(
        on_device, mesh=grid, in_specs=in_specs, out_specs=out_specs, check_vma=False
    )
```

```python
import jax
import jax.numpy as jnp
from jax import lax
from jax.experimental import pallas as pl
from jax.experimental.pallas import tpu as pltpu
from jax.sharding import Mesh, PartitionSpec as P

LEVELS = 4
PLANE = ("x", "y")
F32, BF16 = jnp.float32, jnp.bfloat16


def matmul(a, b, form):
    dims = {"nn": (((1,), (0,)), ((), ())), "nt": (((1,), (1,)), ((), ()))}[form]
    return lax.dot_general(a, b, dims, preferred_element_type=F32)


def split(value):
    high = value.astype(BF16)
    return high, (value - high.astype(F32)).astype(BF16)


class Far:
    def __init__(self, array):
        self.array = array


def call(body, outs, *args, scratch=()):
    vmem = pl.BlockSpec(memory_space=pltpu.VMEM)
    in_specs, given = [], []
    for arg in args:
        if isinstance(arg, Far):
            in_specs.append(pl.BlockSpec(memory_space=pltpu.HBM))
            given.append(pltpu.with_memory_space_constraint(arg.array, pltpu.HBM))
        else:
            in_specs.append(vmem)
            given.append(pltpu.with_memory_space_constraint(arg, pltpu.VMEM))
    return pl.pallas_call(
        body,
        out_shape=[out if isinstance(out, jax.ShapeDtypeStruct) else pltpu.VMEM(*out) for out in outs],
        in_specs=in_specs,
        out_specs=[vmem] * len(outs),
        scratch_shapes=list(scratch),
        compiler_params=pltpu.CompilerParams(vmem_limit_bytes=8 << 20),
    )(*given)


def send_to_all(out_ref, value):
    value = value.astype(BF16)
    for slot in range(out_ref.shape[0]):
        out_ref[slot] = value


def sum_slots(ref):
    total = ref[0].astype(F32)
    for slot in range(1, ref.shape[0]):
        total = total + ref[slot].astype(F32)
    return total


def packed(value):
    half = value.shape[1] // 2
    return jnp.concatenate([value[:, :half], value[:, half:]], axis=0)


def unpacked(value):
    rows = value.shape[0] // 2
    return jnp.concatenate([value[:rows], value[rows:]], axis=1)


def solve(value, high_ref, low_ref, form):
    rows, block = value.shape[0], high_ref.shape[1]
    out = []
    for p in range(high_ref.shape[0]):
        panel = value[:, p * block : (p + 1) * block]
        top = panel.astype(BF16).astype(F32)
        both = jnp.concatenate([top, panel - top], axis=0).astype(BF16)
        product = matmul(both, high_ref[p], form) + matmul(both, low_ref[p], form)
        out.append(product[:rows] + product[rows:])
    return jnp.concatenate(out, axis=1)


def start_kernel(
    order_hbm, load_hbm, inverse_hbm, front_hbm, modes_hbm,
    level_ref, high_ref, low_ref, mine_ref, y_ref, send_ref, front_ref, modes_ref,
    order_ref, load_ref, inverse_ref, sems,
):
    panels, block = high_ref.shape[0], high_ref.shape[1]
    vectors = load_ref.shape[0] // 2
    copies = [
        pltpu.make_async_copy(order_hbm, order_ref, sems.at[0]),
        pltpu.make_async_copy(load_hbm, load_ref, sems.at[1]),
        pltpu.make_async_copy(inverse_hbm, inverse_ref, sems.at[2]),
        pltpu.make_async_copy(front_hbm, front_ref, sems.at[3]),
        pltpu.make_async_copy(modes_hbm, modes_ref, sems.at[4]),
    ]
    for copy in copies:
        copy.start()
    copies[0].wait()
    order = jnp.broadcast_to(order_ref[...], (panels, order_ref.shape[1]))
    per_level = order.shape[1] // LEVELS
    names = lax.axis_index(PLANE) * panels + lax.broadcasted_iota(jnp.int32, order.shape, 0)
    counting = lax.broadcasted_iota(jnp.int32, order.shape, 1)
    ranks = jnp.sum(jnp.where(order == names, counting, 0), axis=1, keepdims=True)
    levels = jnp.zeros_like(ranks)
    for bound in range(1, LEVELS):
        levels = levels + jnp.where(ranks >= bound * per_level, 1, 0)
    levels = jnp.broadcast_to(levels, (panels, block))
    level_row = jnp.concatenate(
        [jnp.broadcast_to(levels[p : p + 1], (vectors, block)) for p in range(panels)], axis=1
    )
    level_ref[...] = level_row
    copies[1].wait()
    load = jnp.where(lax.axis_index("k") == 0, load_ref[:vectors], load_ref[vectors:])
    mine_ref[...] = load
    copies[2].wait()
    high, low = split(inverse_ref[...])
    high_ref[...] = high
    low_ref[...] = low
    y = jnp.where(level_row == 0, solve(load, high_ref, low_ref, "nt"), 0.0)
    y_ref[...] = y
    send_to_all(send_ref, packed(y))
    copies[3].wait()
    copies[4].wait()


def update_kernel(first, last, front_ref, partner_ref, got_ref, *refs):
    got = got_ref[lax.axis_index("z")]
    rows = got.shape[0] // 2
    own, other = matmul(got, front_ref[...], "nt"), matmul(got, partner_ref[...], "nt")
    out = jnp.where(lax.axis_index("k") == 0, own[:rows] + other[rows:], own[rows:] + other[:rows])
    if not first:
        out = refs[0][...] + out
    if not last:
        refs[-2][...] = out
    send_to_all(refs[-1], packed(out))


def forward_kernel(level, got_ref, mine_ref, level_ref, high_ref, low_ref, y_in_ref, y_ref, send_ref):
    chosen = level_ref[...] == level
    candidate = solve(mine_ref[...] - unpacked(sum_slots(got_ref)), high_ref, low_ref, "nt")
    y_ref[...] = jnp.where(chosen, candidate, y_in_ref[...])
    send_to_all(send_ref, packed(jnp.where(chosen, candidate, 0.0)))


def back_product(x, front_ref, partner_ref):
    x = x.astype(BF16)
    own, other = matmul(x, front_ref[...], "nn"), matmul(x, partner_ref[...], "nn")
    first = lax.axis_index("k") == 0
    return jnp.concatenate([jnp.where(first, own, other), jnp.where(first, other, own)], axis=0)


def turn_kernel(
    front_ref, partner_ref, got_ref, mine_ref, level_ref, high_ref, low_ref, y_in_ref,
    y_ref, x_ref, pending_ref, send_ref,
):
    chosen = level_ref[...] == LEVELS - 1
    candidate = solve(mine_ref[...] - unpacked(sum_slots(got_ref)), high_ref, low_ref, "nt")
    y = jnp.where(chosen, candidate, y_in_ref[...])
    y_ref[...] = y
    x = jnp.where(chosen, solve(y, high_ref, low_ref, "nn"), 0.0)
    x_ref[...] = packed(x)
    out = back_product(x, front_ref, partner_ref)
    pending_ref[...] = out
    send_to_all(send_ref, out)


def back_kernel(level, got_ref, level_ref, high_ref, low_ref, y_ref, send_ref):
    x = solve(y_ref[...] - unpacked(sum_slots(got_ref)), high_ref, low_ref, "nn")
    send_to_all(send_ref, packed(jnp.where(level_ref[...] == level, x, 0.0)))


def back_update_kernel(last, front_ref, partner_ref, got_ref, x_in_ref, pending_in_ref, x_ref, *refs):
    fresh = got_ref[lax.axis_index(PLANE)].astype(F32)
    x_ref[...] = x_in_ref[...] + fresh
    out = pending_in_ref[...] + back_product(unpacked(fresh), front_ref, partner_ref)
    if not last:
        refs[0][...] = out
    send_to_all(refs[-1], out)


def last_pick_kernel(got_ref, x_in_ref, x_ref):
    x_ref[...] = x_in_ref[...] + got_ref[lax.axis_index(PLANE)].astype(F32)


def coords_kernel(pair_ref, tie_ref, mass_ref, modes_ref, x_ref, static_ref, send_ref):
    x = jnp.concatenate([unpacked(pair_ref[0]), unpacked(pair_ref[1])], axis=0)
    x_ref[...] = x
    static = tie_ref[...] * x
    static_ref[...] = static
    coords = matmul((mass_ref[...] * static).astype(BF16), modes_ref[...], "nt").astype(BF16)
    cores, half = 2, send_ref.shape[2]
    for slot in range(send_ref.shape[0]):
        part = slot % cores
        send_ref[slot] = coords[:, part * half : (part + 1) * half]


def relay_kernel(got_ref, send_ref):
    send_to_all(send_ref, sum_slots(got_ref))


def gathered_kernel(got_ref, out_ref):
    out_ref[...] = sum_slots(got_ref).astype(BF16)


def finish_kernel(static_ref, pair_ref, modes_ref, x_ref, whole_ref, out_ref):
    half = pair_ref.shape[2]
    correction = matmul(pair_ref[0], modes_ref[:half], "nn") + matmul(pair_ref[1], modes_ref[half:], "nn")
    whole_ref[...] = x_ref[...]
    out_ref[:, 0, :] = static_ref[...] - correction


def bound(body, *settings):
    def kernel(*refs):
        body(*settings, *refs)

    return kernel


def on_device(front, diag_inverse, load, panel_order, tie, mass, modes):
    vectors = load.shape[0]
    rows, half = front.shape
    plane = lax.axis_size(PLANE)
    depth = lax.axis_size("z")
    cores = lax.axis_size("k")
    mode_rows = modes.reshape(modes.shape[0], -1)

    flat = (vectors // cores, rows)
    small = ((vectors, half), F32)
    narrow = ((vectors, half), BF16)
    to_plane = ((plane, vectors, half), BF16)
    to_depth = ((depth, vectors, half), BF16)
    inverse_part = (diag_inverse.shape, BF16)

    def exchange(value, axes):
        return lax.all_to_all(value, axes, 0, 0, tiled=True)

    def both_cores(value):
        return lax.all_gather(value, "k", axis=0)

    partner = lax.ppermute(front, "k", [(core, 1 - core) for core in range(cores)])
    level_row, high, low, mine, y, send, front, mode_rows = call(
        start_kernel,
        [(flat, jnp.int32), inverse_part, inverse_part, (flat, F32), (flat, F32), to_plane,
         (front.shape, BF16), (mode_rows.shape, BF16)],
        Far(panel_order[None, :]), Far(load), Far(diag_inverse), Far(front), Far(mode_rows),
        scratch=[
            pltpu.VMEM((1, panel_order.shape[0]), jnp.int32),
            pltpu.VMEM(load.shape, F32),
            pltpu.VMEM(diag_inverse.shape, F32),
            pltpu.SemaphoreType.DMA((5,)),
        ],
    )
    pending = ()
    for level in range(1, LEVELS):
        last = level == LEVELS - 1
        *pending, send = call(
            bound(update_kernel, not pending, last),
            [to_depth] if last else [(flat, F32), to_depth],
            front, partner, exchange(send, PLANE), *pending,
        )
        args = (exchange(send, "z"), mine, level_row, high, low, y)
        if not last:
            y, send = call(bound(forward_kernel, level), [(flat, F32), to_plane], *args)
    y, x, pending, send = call(turn_kernel, [(flat, F32), small, small, to_plane], front, partner, *args)

    for level in reversed(range(LEVELS - 1)):
        (send,) = call(bound(back_kernel, level), [to_depth], exchange(send, PLANE), level_row, high, low, y)
        got = exchange(send, "z")
        if level > 0:
            last = level == 1
            x, *rest, send = call(
                bound(back_update_kernel, last),
                [small, to_plane] if last else [small, small, to_plane],
                front, partner, got, x, pending,
            )
            pending = None if last else rest[0]
        else:
            (x,) = call(last_pick_kernel, [small], got, x)

    whole, static, send = call(
        coords_kernel,
        [((vectors, rows), F32), ((vectors, rows), F32), ((plane * cores, vectors, half), BF16)],
        both_cores(x), tie, mass, mode_rows,
    )
    (send,) = call(relay_kernel, [to_depth], exchange(send, PLANE + ("k",)))
    (coords,) = call(gathered_kernel, [narrow], exchange(send, "z"))
    return tuple(
        call(
            finish_kernel,
            [jax.ShapeDtypeStruct((vectors, rows), F32), jax.ShapeDtypeStruct((vectors, 1, rows), F32)],
            static, both_cores(coords), mode_rows, whole,
        )
    )


def solution(mesh):
    grid = Mesh(mesh.devices.reshape(4, 4, 16, 2), PLANE + ("z", "k"))
    row, col = PLANE, ("z", "k")
    in_specs = (
        P(row, col),
        P(row, None, None),
        P(None, row),
        P(),
        P(col, row),
        P(col, row),
        P(None, col, row),
    )
    out_specs = (P(None, row), P(None, col, row))
    return jax.shard_map(
        on_device, mesh=grid, in_specs=in_specs, out_specs=out_specs, check_vma=False
    )
```

```python
import jax
import jax.numpy as jnp
from jax import lax
from jax.experimental import pallas as pl
from jax.experimental.pallas import tpu as pltpu
from jax.sharding import Mesh, PartitionSpec as P


LEVELS = 4
ROOM = (4, 5, 6)
PLANE = ("x", "y")
F32, BF16 = jnp.float32, jnp.bfloat16


def matmul(a, b, form):
    dims = {"nn": (((1,), (0,)), ((), ())), "nt": (((1,), (1,)), ((), ()))}[form]
    return lax.dot_general(a, b, dims, preferred_element_type=F32)


def split(value):
    high = value.astype(BF16)
    return high, (value - high.astype(F32)).astype(BF16)


class Far:
    def __init__(self, array):
        self.array = array


def call(body, outs, *args, scratch=()):
    vmem = pl.BlockSpec(memory_space=pltpu.VMEM)
    in_specs, given = [], []
    for arg in args:
        if isinstance(arg, Far):
            in_specs.append(pl.BlockSpec(memory_space=pltpu.HBM))
            given.append(pltpu.with_memory_space_constraint(arg.array, pltpu.HBM))
        else:
            in_specs.append(vmem)
            given.append(pltpu.with_memory_space_constraint(arg, pltpu.VMEM))
    return pl.pallas_call(
        body,
        out_shape=[out if isinstance(out, jax.ShapeDtypeStruct) else pltpu.VMEM(*out) for out in outs],
        in_specs=in_specs,
        out_specs=[vmem] * len(outs),
        scratch_shapes=list(scratch),
        compiler_params=pltpu.CompilerParams(vmem_limit_bytes=8 << 20),
    )(*given)


def send_to_all(out_ref, value):
    value = value.astype(BF16)
    for slot in range(out_ref.shape[0]):
        out_ref[slot] = value


def sum_slots(ref):
    total = ref[0].astype(F32)
    for slot in range(1, ref.shape[0]):
        total = total + ref[slot].astype(F32)
    return total


def pick(value, code, first, room):
    block = 128
    panels = value.shape[1] // block
    out = []
    for j in range(room):
        total = None
        for p in range(panels):
            at = slice(p * block, (p + 1) * block)
            part = jnp.where(code[:, at] == first + j, value[:, at], 0.0)
            total = part if total is None else total + part
        out.append(total)
    return jnp.concatenate(out, axis=1)


def place(value, code, first, room):
    block = 128
    panels = code.shape[1] // block
    out = []
    for p in range(panels):
        at = slice(p * block, (p + 1) * block)
        total = jnp.zeros((code.shape[0], block), F32)
        for j in range(room):
            total = total + jnp.where(code[:, at] == first + j, value[:, j * block : (j + 1) * block], 0.0)
        out.append(total)
    return jnp.concatenate(out, axis=1)


def solve(value, high_ref, low_ref, form):
    rows, block = value.shape[0], high_ref.shape[1]
    out = []
    for p in range(high_ref.shape[0]):
        panel = value[:, p * block : (p + 1) * block]
        top = panel.astype(BF16).astype(F32)
        both = jnp.concatenate([top, panel - top], axis=0).astype(BF16)
        product = matmul(both, high_ref[p], form) + matmul(both, low_ref[p], form)
        out.append(product[:rows] + product[rows:])
    return jnp.concatenate(out, axis=1)


def in_level(code, level, panels):
    return (code >= level * panels) & (code < (level + 1) * panels)


def start_kernel(
    order_hbm, load_hbm, inverse_hbm, front_hbm,
    row_code_ref, col_code_ref, high_ref, low_ref, mine_ref, y_ref, send_ref, front_ref,
    order_ref, load_ref, inverse_ref, sems,
):
    panels, block = high_ref.shape[0], high_ref.shape[1]
    vectors = load_ref.shape[0] // 2
    copies = [
        pltpu.make_async_copy(order_hbm, order_ref, sems.at[0]),
        pltpu.make_async_copy(load_hbm, load_ref, sems.at[1]),
        pltpu.make_async_copy(inverse_hbm, inverse_ref, sems.at[2]),
        pltpu.make_async_copy(front_hbm, front_ref, sems.at[3]),
    ]
    for copy in copies:
        copy.start()
    copies[0].wait()
    order = jnp.broadcast_to(order_ref[...], (2 * panels, order_ref.shape[1]))
    per_level = order.shape[1] // LEVELS
    panel = lax.broadcasted_iota(jnp.int32, order.shape, 0)
    of_rows = panel < panels
    place_in = jnp.where(of_rows, panel, panel - panels)
    names = jnp.where(of_rows, lax.axis_index(PLANE), lax.axis_index("z")) * panels + place_in
    counting = lax.broadcasted_iota(jnp.int32, order.shape, 1)
    ranks = jnp.sum(jnp.where(order == names, counting, 0), axis=1, keepdims=True)
    levels = jnp.zeros_like(ranks)
    for bound in range(1, LEVELS):
        levels = levels + jnp.where(ranks >= bound * per_level, 1, 0)
    levels = jnp.broadcast_to(levels, order.shape)
    codes = levels * panels
    for p in range(panels - 1):
        same = levels == jnp.where(of_rows, levels[p : p + 1], levels[panels + p : panels + p + 1])
        codes = codes + jnp.where(same & (place_in > p), 1, 0)
    spread_codes = [jnp.broadcast_to(codes[p : p + 1], (vectors, block)) for p in range(2 * panels)]
    row_code = jnp.concatenate(spread_codes[:panels], axis=1)
    row_code_ref[...] = row_code
    col_code_ref[...] = jnp.concatenate(spread_codes[panels:], axis=1)
    copies[1].wait()
    load = jnp.where(lax.axis_index("k") == 0, load_ref[:vectors], load_ref[vectors:])
    mine_ref[...] = load
    copies[2].wait()
    high, low = split(inverse_ref[...])
    high_ref[...] = high
    low_ref[...] = low
    y = jnp.where(in_level(row_code, 0, panels), solve(load, high_ref, low_ref, "nt"), 0.0)
    y_ref[...] = y
    send_to_all(send_ref, y)
    copies[3].wait()


def update_kernel(level, room, front_ref, partner_ref, got_ref, row_code_ref, col_code_ref, *refs):
    first, last = level == 1, level == LEVELS - 1
    got = got_ref[lax.axis_index("z")]
    if not first:
        got = place(got.astype(F32), col_code_ref[...], (level - 1) * 8, room).astype(BF16)
    half = front_ref.shape[1]
    left, right = got[:, :half], got[:, half:]
    on_left = lax.axis_index("k") == 0
    out = matmul(jnp.where(on_left, left, right), front_ref[...], "nt") + matmul(
        jnp.where(on_left, right, left), partner_ref[...], "nt"
    )
    if not first:
        out = refs[0][...] + out
    if not last:
        refs[-2][...] = out
    send_to_all(refs[-1], pick(out, row_code_ref[...], level * 8, room))


def forward_step(level, room, got_ref, mine_ref, code, high_ref, low_ref):
    return solve(mine_ref[...] - place(sum_slots(got_ref), code, level * 8, room), high_ref, low_ref, "nt")


def forward_kernel(level, room, got_ref, mine_ref, row_code_ref, high_ref, low_ref, y_in_ref, y_ref, send_ref):
    code = row_code_ref[...]
    candidate = forward_step(level, room, got_ref, mine_ref, code, high_ref, low_ref)
    y_ref[...] = jnp.where(in_level(code, level, 8), candidate, y_in_ref[...])
    send_to_all(send_ref, pick(candidate, code, level * 8, room))


def back_product(x, front_ref, partner_ref):
    x = x.astype(BF16)
    own, other = matmul(x, front_ref[...], "nn"), matmul(x, partner_ref[...], "nn")
    first = lax.axis_index("k") == 0
    return jnp.concatenate([jnp.where(first, own, other), jnp.where(first, other, own)], axis=1)


def turn_kernel(
    room, front_ref, partner_ref, got_ref, mine_ref, row_code_ref, col_code_ref, high_ref, low_ref, y_in_ref,
    modes_hbm, y_ref, x_ref, pending_ref, send_ref, modes_ref, sem,
):
    modes_copy = pltpu.make_async_copy(modes_hbm, modes_ref, sem)
    modes_copy.start()
    code = row_code_ref[...]
    level = LEVELS - 1
    chosen = in_level(code, level, 8)
    candidate = forward_step(level, room, got_ref, mine_ref, code, high_ref, low_ref)
    y = jnp.where(chosen, candidate, y_in_ref[...])
    y_ref[...] = y
    x = jnp.where(chosen, solve(y, high_ref, low_ref, "nn"), 0.0)
    x_ref[...] = x
    out = back_product(x, front_ref, partner_ref)
    pending_ref[...] = out
    send_to_all(send_ref, pick(out, col_code_ref[...], (level - 1) * 8, room))
    modes_copy.wait()


def back_kernel(level, room, got_ref, col_code_ref, high_ref, low_ref, y_ref, send_ref):
    code = col_code_ref[...]
    here = place(sum_slots(got_ref), code, level * 8, room)
    send_to_all(send_ref, pick(solve(y_ref[...] - here, high_ref, low_ref, "nn"), code, level * 8, room))


def fresh_rows(level, room, got_ref, row_code_ref):
    got = got_ref[lax.axis_index(PLANE)].astype(F32)
    return place(got, row_code_ref[...], level * 8, room)


def back_update_kernel(
    level, room, front_ref, partner_ref, got_ref, row_code_ref, col_code_ref, x_in_ref, pending_in_ref, x_ref, *refs
):
    fresh = fresh_rows(level, room, got_ref, row_code_ref)
    x_ref[...] = x_in_ref[...] + fresh
    out = pending_in_ref[...] + back_product(fresh, front_ref, partner_ref)
    if level > 1:
        refs[0][...] = out
    send_to_all(refs[-1], pick(out, col_code_ref[...], (level - 1) * 8, room))


def last_pick_kernel(room, got_ref, row_code_ref, x_in_ref, x_ref):
    x_ref[...] = x_in_ref[...] + fresh_rows(0, room, got_ref, row_code_ref)


def coords_kernel(pair_ref, tie_ref, mass_ref, modes_ref, x_ref, static_ref, send_ref):
    x = jnp.concatenate([pair_ref[0], pair_ref[1]], axis=0)
    x_ref[...] = x
    static = tie_ref[...] * x
    static_ref[...] = static
    coords = matmul((mass_ref[...] * static).astype(BF16), modes_ref[...], "nt").astype(BF16)
    cores, half = 2, send_ref.shape[2]
    for slot in range(send_ref.shape[0]):
        part = slot % cores
        send_ref[slot] = coords[:, part * half : (part + 1) * half]


def relay_kernel(got_ref, send_ref):
    send_to_all(send_ref, sum_slots(got_ref))


def gathered_kernel(got_ref, out_ref):
    out_ref[...] = sum_slots(got_ref).astype(BF16)


def finish_kernel(static_ref, pair_ref, modes_ref, x_ref, whole_ref, out_ref):
    half = pair_ref.shape[2]
    correction = matmul(pair_ref[0], modes_ref[:half], "nn") + matmul(pair_ref[1], modes_ref[half:], "nn")
    whole_ref[...] = x_ref[...]
    out_ref[:, 0, :] = static_ref[...] - correction


def bound(body, *settings):
    def kernel(*refs):
        return body(*settings, *refs)

    return kernel


def on_device(front, diag_inverse, load, panel_order, tie, mass, modes):
    vectors = load.shape[0]
    rows, half = front.shape
    plane = lax.axis_size(PLANE)
    depth = lax.axis_size("z")
    cores = lax.axis_size("k")
    mode_rows = modes.reshape(modes.shape[0], -1)

    part = vectors // cores
    panels, block = diag_inverse.shape[0], diag_inverse.shape[1]
    flat = ((part, rows), F32)
    coded = ((part, rows), jnp.int32)
    inverse_part = (diag_inverse.shape, BF16)
    narrow = ((vectors, half), BF16)
    to_depth = ((depth, vectors, half), BF16)

    def exchange(value, axes):
        return lax.all_to_all(value, axes, 0, 0, tiled=True)

    def both_cores(value):
        return lax.all_gather(value, "k", axis=0)

    row_code, col_code, high, low, mine, y, send, front = call(
        start_kernel,
        [coded, coded, inverse_part, inverse_part, flat, flat, ((plane, part, rows), BF16),
         (front.shape, BF16)],
        Far(panel_order[None, :]), Far(load), Far(diag_inverse), Far(front),
        scratch=[
            pltpu.VMEM((1, panel_order.shape[0]), jnp.int32),
            pltpu.VMEM(load.shape, F32),
            pltpu.VMEM(diag_inverse.shape, F32),
            pltpu.SemaphoreType.DMA((4,)),
        ],
    )

    got = exchange(send, PLANE)
    partner = lax.ppermute(front, "k", [(core, 1 - core) for core in range(cores)])

    def solve_levels(room, front, partner, got, row_code, col_code, high, low, mine, y, mode_rows):
        mode_shape = mode_rows.shape
        slots = ((plane, part, room * block), BF16)
        deep = ((depth, part, room * block), BF16)
        pending = ()
        for level in range(1, LEVELS):
            last = level == LEVELS - 1
            *pending, send = call(
                bound(update_kernel, level, room),
                [deep] if last else [flat, deep],
                front, partner, got, row_code, col_code, *pending,
            )
            got = exchange(send, "z")
            if not last:
                y, send = call(
                    bound(forward_kernel, level, room), [flat, slots], got, mine, row_code, high, low, y
                )
                got = exchange(send, PLANE)
        y, x, pending, send, mode_rows = call(
            bound(turn_kernel, room), [flat, flat, flat, slots, (mode_shape, BF16)],
            front, partner, got, mine, row_code, col_code, high, low, y, Far(mode_rows),
            scratch=[pltpu.SemaphoreType.DMA(())],
        )
        for level in reversed(range(LEVELS - 1)):
            (send,) = call(
                bound(back_kernel, level, room), [deep], exchange(send, PLANE), col_code, high, low, y
            )
            got = exchange(send, "z")
            if level > 0:
                x, *rest, send = call(
                    bound(back_update_kernel, level, room),
                    [flat, flat, slots] if level > 1 else [flat, slots],
                    front, partner, got, row_code, col_code, x, pending,
                )
                pending = rest[0] if rest else None
            else:
                (x,) = call(bound(last_pick_kernel, room), [flat], got, row_code, x)
        return x, mode_rows

    blocks = jnp.arange(plane, dtype=jnp.int32)
    inside = (panel_order.reshape(LEVELS, -1, 1) // panels) == blocks
    most = jnp.max(jnp.sum(inside.astype(jnp.int32), axis=1))
    rooms = ROOM + (panels,)
    choice = sum((most > room).astype(jnp.int32) for room in ROOM)
    x, mode_rows = lax.switch(
        choice,
        [bound(solve_levels, room) for room in rooms],
        front, partner, got, row_code, col_code, high, low, mine, y, mode_rows,
    )

    whole, static, send = call(
        coords_kernel,
        [((vectors, rows), F32), ((vectors, rows), F32), ((plane * cores, vectors, half), BF16)],
        both_cores(x), tie, mass, mode_rows,
    )
    (send,) = call(relay_kernel, [to_depth], exchange(send, PLANE + ("k",)))
    (coords,) = call(gathered_kernel, [narrow], exchange(send, "z"))
    return tuple(
        call(
            finish_kernel,
            [jax.ShapeDtypeStruct((vectors, rows), F32), jax.ShapeDtypeStruct((vectors, 1, rows), F32)],
            static, both_cores(coords), mode_rows, whole,
        )
    )


def solution(mesh):
    grid = Mesh(mesh.devices.reshape(4, 4, 16, 2), PLANE + ("z", "k"))
    row, col = PLANE, ("z", "k")
    in_specs = (
        P(row, col),
        P(row, None, None),
        P(None, row),
        P(),
        P(col, row),
        P(col, row),
        P(None, col, row),
    )
    out_specs = (P(None, row), P(None, col, row))
    return jax.shard_map(on_device, mesh=grid, in_specs=in_specs, out_specs=out_specs, check_vma=False)
```

```python
import jax
import jax.numpy as jnp
from jax import lax
from jax.experimental import pallas as pl
from jax.experimental.pallas import tpu as pltpu
from jax.sharding import Mesh, PartitionSpec as P


LEVELS = 4
ROOM = (4, 5, 6)
PLANE = ("x", "y")
F32, BF16 = jnp.float32, jnp.bfloat16


def matmul(a, b, form):
    dims = {"nn": (((1,), (0,)), ((), ())), "nt": (((1,), (1,)), ((), ()))}[form]
    return lax.dot_general(a, b, dims, preferred_element_type=F32)


def split(value):
    high = value.astype(BF16)
    return high, (value - high.astype(F32)).astype(BF16)


CHOICE = pltpu.SMEM((1,), jnp.int32)


class Far:
    def __init__(self, array):
        self.array = array


def call(body, outs, *args, scratch=()):
    vmem = pl.BlockSpec(memory_space=pltpu.VMEM)
    in_specs, given = [], []
    for arg in args:
        if isinstance(arg, Far):
            in_specs.append(pl.BlockSpec(memory_space=pltpu.HBM))
            given.append(pltpu.with_memory_space_constraint(arg.array, pltpu.HBM))
        else:
            in_specs.append(vmem)
            given.append(pltpu.with_memory_space_constraint(arg, pltpu.VMEM))
    return pl.pallas_call(
        body,
        out_shape=[pltpu.VMEM(*out) if isinstance(out, tuple) else out for out in outs],
        in_specs=in_specs,
        out_specs=[pl.BlockSpec(memory_space=pltpu.SMEM) if out is CHOICE else vmem for out in outs],
        scratch_shapes=list(scratch),
        compiler_params=pltpu.CompilerParams(vmem_limit_bytes=8 << 20),
    )(*given)


def send_to_all(out_ref, value):
    value = value.astype(BF16)
    for slot in range(out_ref.shape[0]):
        out_ref[slot] = value


def sum_slots(ref):
    total = ref[0].astype(F32)
    for slot in range(1, ref.shape[0]):
        total = total + ref[slot].astype(F32)
    return total


def pick(value, code, first, room):
    block = 128
    panels = value.shape[1] // block
    out = []
    for j in range(room):
        total = None
        for p in range(panels):
            at = slice(p * block, (p + 1) * block)
            part = jnp.where(code[:, at] == first + j, value[:, at], 0.0)
            total = part if total is None else total + part
        out.append(total)
    return jnp.concatenate(out, axis=1)


def place(value, code, first, room):
    block = 128
    panels = code.shape[1] // block
    out = []
    for p in range(panels):
        at = slice(p * block, (p + 1) * block)
        total = jnp.zeros((code.shape[0], block), F32)
        for j in range(room):
            total = total + jnp.where(code[:, at] == first + j, value[:, j * block : (j + 1) * block], 0.0)
        out.append(total)
    return jnp.concatenate(out, axis=1)


def solve(value, high_ref, low_ref, form):
    rows, block = value.shape[0], high_ref.shape[1]
    out = []
    for p in range(high_ref.shape[0]):
        panel = value[:, p * block : (p + 1) * block]
        top = panel.astype(BF16).astype(F32)
        both = jnp.concatenate([top, panel - top], axis=0).astype(BF16)
        product = matmul(both, high_ref[p], form) + matmul(both, low_ref[p], form)
        out.append(product[:rows] + product[rows:])
    return jnp.concatenate(out, axis=1)


def in_level(code, level, panels):
    return (code >= level * panels) & (code < (level + 1) * panels)


def start_kernel(
    order_hbm, load_hbm, inverse_hbm, front_hbm,
    row_code_ref, col_code_ref, high_ref, low_ref, mine_ref, y_ref, send_ref, front_ref, choice_ref,
    order_ref, load_ref, inverse_ref, sems,
):
    panels, block = high_ref.shape[0], high_ref.shape[1]
    vectors = load_ref.shape[0] // 2
    copies = [
        pltpu.make_async_copy(order_hbm, order_ref, sems.at[0]),
        pltpu.make_async_copy(load_hbm, load_ref, sems.at[1]),
        pltpu.make_async_copy(inverse_hbm, inverse_ref, sems.at[2]),
        pltpu.make_async_copy(front_hbm, front_ref, sems.at[3]),
    ]
    for copy in copies:
        copy.start()
    copies[0].wait()
    order = jnp.broadcast_to(order_ref[...], (2 * panels, order_ref.shape[1]))
    per_level = order.shape[1] // LEVELS
    panel = lax.broadcasted_iota(jnp.int32, order.shape, 0)
    of_rows = panel < panels
    place_in = jnp.where(of_rows, panel, panel - panels)
    names = jnp.where(of_rows, lax.axis_index(PLANE), lax.axis_index("z")) * panels + place_in
    counting = lax.broadcasted_iota(jnp.int32, order.shape, 1)
    ranks = jnp.sum(jnp.where(order == names, counting, 0), axis=1, keepdims=True)
    levels = jnp.zeros_like(ranks)
    for bound in range(1, LEVELS):
        levels = levels + jnp.where(ranks >= bound * per_level, 1, 0)
    levels = jnp.broadcast_to(levels, order.shape)
    codes = levels * panels
    for p in range(panels - 1):
        same = levels == jnp.where(of_rows, levels[p : p + 1], levels[panels + p : panels + p + 1])
        codes = codes + jnp.where(same & (place_in > p), 1, 0)
    spread_codes = [jnp.broadcast_to(codes[p : p + 1], (vectors, block)) for p in range(2 * panels)]
    row_code = jnp.concatenate(spread_codes[:panels], axis=1)
    row_code_ref[...] = row_code
    col_code_ref[...] = jnp.concatenate(spread_codes[panels:], axis=1)
    inside = order // panels == panel
    most = jnp.zeros((2 * panels, 1), jnp.int32)
    for level in range(LEVELS):
        of_level = inside & (counting >= level * per_level) & (counting < (level + 1) * per_level)
        most = jnp.maximum(most, jnp.sum(jnp.where(of_level, 1, 0), axis=1, keepdims=True))
    choice = jnp.zeros_like(most)
    for room in ROOM:
        choice = choice + jnp.where(most > room, 1, 0)
    choice_ref[0] = jnp.max(choice)
    copies[1].wait()
    load = jnp.where(lax.axis_index("k") == 0, load_ref[:vectors], load_ref[vectors:])
    mine_ref[...] = load
    copies[2].wait()
    high, low = split(inverse_ref[...])
    high_ref[...] = high
    low_ref[...] = low
    y = jnp.where(in_level(row_code, 0, panels), solve(load, high_ref, low_ref, "nt"), 0.0)
    y_ref[...] = y
    send_to_all(send_ref, y)
    copies[3].wait()


def update_kernel(level, room, front_ref, partner_ref, got_ref, row_code_ref, col_code_ref, *refs):
    first, last = level == 1, level == LEVELS - 1
    got = got_ref[lax.axis_index("z")]
    if not first:
        got = place(got.astype(F32), col_code_ref[...], (level - 1) * 8, room).astype(BF16)
    half = front_ref.shape[1]
    left, right = got[:, :half], got[:, half:]
    on_left = lax.axis_index("k") == 0
    out = matmul(jnp.where(on_left, left, right), front_ref[...], "nt") + matmul(
        jnp.where(on_left, right, left), partner_ref[...], "nt"
    )
    if not first:
        out = refs[0][...] + out
    if not last:
        refs[-2][...] = out
    send_to_all(refs[-1], pick(out, row_code_ref[...], level * 8, room))


def forward_step(level, room, got_ref, mine_ref, code, high_ref, low_ref):
    return solve(mine_ref[...] - place(sum_slots(got_ref), code, level * 8, room), high_ref, low_ref, "nt")


def forward_kernel(level, room, got_ref, mine_ref, row_code_ref, high_ref, low_ref, y_in_ref, y_ref, send_ref):
    code = row_code_ref[...]
    candidate = forward_step(level, room, got_ref, mine_ref, code, high_ref, low_ref)
    y_ref[...] = jnp.where(in_level(code, level, 8), candidate, y_in_ref[...])
    send_to_all(send_ref, pick(candidate, code, level * 8, room))


def back_product(x, front_ref, partner_ref):
    x = x.astype(BF16)
    own, other = matmul(x, front_ref[...], "nn"), matmul(x, partner_ref[...], "nn")
    first = lax.axis_index("k") == 0
    return jnp.concatenate([jnp.where(first, own, other), jnp.where(first, other, own)], axis=1)


def turn_kernel(
    room, front_ref, partner_ref, got_ref, mine_ref, row_code_ref, col_code_ref, high_ref, low_ref, y_in_ref,
    modes_hbm, y_ref, x_ref, pending_ref, send_ref, modes_ref, sem,
):
    modes_copy = pltpu.make_async_copy(modes_hbm, modes_ref, sem)
    modes_copy.start()
    code = row_code_ref[...]
    level = LEVELS - 1
    chosen = in_level(code, level, 8)
    candidate = forward_step(level, room, got_ref, mine_ref, code, high_ref, low_ref)
    y = jnp.where(chosen, candidate, y_in_ref[...])
    y_ref[...] = y
    x = jnp.where(chosen, solve(y, high_ref, low_ref, "nn"), 0.0)
    x_ref[...] = x
    out = back_product(x, front_ref, partner_ref)
    pending_ref[...] = out
    send_to_all(send_ref, pick(out, col_code_ref[...], (level - 1) * 8, room))
    modes_copy.wait()


def back_kernel(level, room, got_ref, col_code_ref, high_ref, low_ref, y_ref, send_ref):
    code = col_code_ref[...]
    here = place(sum_slots(got_ref), code, level * 8, room)
    send_to_all(send_ref, pick(solve(y_ref[...] - here, high_ref, low_ref, "nn"), code, level * 8, room))


def fresh_rows(level, room, got_ref, row_code_ref):
    got = got_ref[lax.axis_index(PLANE)].astype(F32)
    return place(got, row_code_ref[...], level * 8, room)


def back_update_kernel(
    level, room, front_ref, partner_ref, got_ref, row_code_ref, col_code_ref, x_in_ref, pending_in_ref, x_ref, *refs
):
    fresh = fresh_rows(level, room, got_ref, row_code_ref)
    x_ref[...] = x_in_ref[...] + fresh
    out = pending_in_ref[...] + back_product(fresh, front_ref, partner_ref)
    if level > 1:
        refs[0][...] = out
    send_to_all(refs[-1], pick(out, col_code_ref[...], (level - 1) * 8, room))


def last_pick_kernel(room, got_ref, row_code_ref, x_in_ref, x_ref):
    x_ref[...] = x_in_ref[...] + fresh_rows(0, room, got_ref, row_code_ref)


def coords_kernel(pair_ref, tie_ref, mass_ref, modes_ref, x_ref, static_ref, send_ref):
    x = jnp.concatenate([pair_ref[0], pair_ref[1]], axis=0)
    x_ref[...] = x
    static = tie_ref[...] * x
    static_ref[...] = static
    coords = matmul((mass_ref[...] * static).astype(BF16), modes_ref[...], "nt").astype(BF16)
    cores, half = 2, send_ref.shape[2]
    for slot in range(send_ref.shape[0]):
        part = slot % cores
        send_ref[slot] = coords[:, part * half : (part + 1) * half]


def relay_kernel(got_ref, send_ref):
    send_to_all(send_ref, sum_slots(got_ref))


def gathered_kernel(got_ref, out_ref):
    out_ref[...] = sum_slots(got_ref).astype(BF16)


def finish_kernel(static_ref, pair_ref, modes_ref, x_ref, whole_ref, out_ref):
    half = pair_ref.shape[2]
    correction = matmul(pair_ref[0], modes_ref[:half], "nn") + matmul(pair_ref[1], modes_ref[half:], "nn")
    whole_ref[...] = x_ref[...]
    out_ref[:, 0, :] = static_ref[...] - correction


def bound(body, *settings):
    def kernel(*refs):
        return body(*settings, *refs)

    return kernel


def on_device(front, diag_inverse, load, panel_order, tie, mass, modes):
    vectors = load.shape[0]
    rows, half = front.shape
    plane = lax.axis_size(PLANE)
    depth = lax.axis_size("z")
    cores = lax.axis_size("k")
    mode_rows = modes.reshape(modes.shape[0], -1)

    part = vectors // cores
    panels, block = diag_inverse.shape[0], diag_inverse.shape[1]
    flat = ((part, rows), F32)
    coded = ((part, rows), jnp.int32)
    inverse_part = (diag_inverse.shape, BF16)
    narrow = ((vectors, half), BF16)
    to_depth = ((depth, vectors, half), BF16)

    def exchange(value, axes):
        return lax.all_to_all(value, axes, 0, 0, tiled=True)

    def both_cores(value):
        return lax.all_gather(value, "k", axis=0)

    row_code, col_code, high, low, mine, y, send, front, choice = call(
        start_kernel,
        [coded, coded, inverse_part, inverse_part, flat, flat, ((plane, part, rows), BF16),
         (front.shape, BF16), CHOICE],
        Far(panel_order[None, :]), Far(load), Far(diag_inverse), Far(front),
        scratch=[
            pltpu.VMEM((1, panel_order.shape[0]), jnp.int32),
            pltpu.VMEM(load.shape, F32),
            pltpu.VMEM(diag_inverse.shape, F32),
            pltpu.SemaphoreType.DMA((4,)),
        ],
    )

    got = exchange(send, PLANE)
    partner = lax.ppermute(front, "k", [(core, 1 - core) for core in range(cores)])

    def solve_levels(room, front, partner, got, row_code, col_code, high, low, mine, y, mode_rows):
        mode_shape = mode_rows.shape
        slots = ((plane, part, room * block), BF16)
        deep = ((depth, part, room * block), BF16)
        pending = ()
        for level in range(1, LEVELS):
            last = level == LEVELS - 1
            *pending, send = call(
                bound(update_kernel, level, room),
                [deep] if last else [flat, deep],
                front, partner, got, row_code, col_code, *pending,
            )
            got = exchange(send, "z")
            if not last:
                y, send = call(
                    bound(forward_kernel, level, room), [flat, slots], got, mine, row_code, high, low, y
                )
                got = exchange(send, PLANE)
        y, x, pending, send, mode_rows = call(
            bound(turn_kernel, room), [flat, flat, flat, slots, (mode_shape, BF16)],
            front, partner, got, mine, row_code, col_code, high, low, y, Far(mode_rows),
            scratch=[pltpu.SemaphoreType.DMA(())],
        )
        for level in reversed(range(LEVELS - 1)):
            (send,) = call(
                bound(back_kernel, level, room), [deep], exchange(send, PLANE), col_code, high, low, y
            )
            got = exchange(send, "z")
            if level > 0:
                x, *rest, send = call(
                    bound(back_update_kernel, level, room),
                    [flat, flat, slots] if level > 1 else [flat, slots],
                    front, partner, got, row_code, col_code, x, pending,
                )
                pending = rest[0] if rest else None
            else:
                (x,) = call(bound(last_pick_kernel, room), [flat], got, row_code, x)
        return x, mode_rows

    rooms = ROOM + (panels,)
    x, mode_rows = lax.switch(
        choice[0],
        [bound(solve_levels, room) for room in rooms],
        front, partner, got, row_code, col_code, high, low, mine, y, mode_rows,
    )

    whole, static, send = call(
        coords_kernel,
        [((vectors, rows), F32), ((vectors, rows), F32), ((plane * cores, vectors, half), BF16)],
        both_cores(x), tie, mass, mode_rows,
    )
    (send,) = call(relay_kernel, [to_depth], exchange(send, PLANE + ("k",)))
    (coords,) = call(gathered_kernel, [narrow], exchange(send, "z"))
    return tuple(
        call(
            finish_kernel,
            [jax.ShapeDtypeStruct((vectors, rows), F32), jax.ShapeDtypeStruct((vectors, 1, rows), F32)],
            static, both_cores(coords), mode_rows, whole,
        )
    )


def solution(mesh):
    grid = Mesh(mesh.devices.reshape(4, 4, 16, 2), PLANE + ("z", "k"))
    row, col = PLANE, ("z", "k")
    in_specs = (
        P(row, col),
        P(row, None, None),
        P(None, row),
        P(),
        P(col, row),
        P(col, row),
        P(None, col, row),
    )
    out_specs = (P(None, row), P(None, col, row))
    return jax.shard_map(on_device, mesh=grid, in_specs=in_specs, out_specs=out_specs, check_vma=False)
```

```python
import jax
import jax.numpy as jnp
from jax import lax
from jax.experimental import pallas as pl
from jax.experimental.pallas import tpu as pltpu
from jax.sharding import Mesh, PartitionSpec as P

LEVELS = 4
ROOM = (4, 5, 6)
PLANE = ("x", "y")
F32, BF16 = jnp.float32, jnp.bfloat16


def matmul(a, b, form):
    dims = {"nn": (((1,), (0,)), ((), ())), "nt": (((1,), (1,)), ((), ()))}[form]
    return lax.dot_general(a, b, dims, preferred_element_type=F32)


def split(value):
    high = value.astype(BF16)
    return high, (value - high.astype(F32)).astype(BF16)


CHOICE = pltpu.SMEM((1,), jnp.int32)


class Far:
    def __init__(self, array):
        self.array = array


def call(body, outs, *args, scratch=()):
    vmem = pl.BlockSpec(memory_space=pltpu.VMEM)
    in_specs, given = [], []
    for arg in args:
        if isinstance(arg, Far):
            in_specs.append(pl.BlockSpec(memory_space=pltpu.HBM))
            given.append(pltpu.with_memory_space_constraint(arg.array, pltpu.HBM))
        else:
            in_specs.append(vmem)
            given.append(pltpu.with_memory_space_constraint(arg, pltpu.VMEM))
    return pl.pallas_call(
        body,
        out_shape=[pltpu.VMEM(*out) if isinstance(out, tuple) else out for out in outs],
        in_specs=in_specs,
        out_specs=[pl.BlockSpec(memory_space=pltpu.SMEM) if out is CHOICE else vmem for out in outs],
        scratch_shapes=list(scratch),
        compiler_params=pltpu.CompilerParams(vmem_limit_bytes=8 << 20),
    )(*given)


def send_to_all(out_ref, value):
    value = value.astype(BF16)
    for slot in range(out_ref.shape[0]):
        out_ref[slot] = value


def sum_slots(ref):
    total = ref[0].astype(F32)
    for slot in range(1, ref.shape[0]):
        total = total + ref[slot].astype(F32)
    return total


def pick(value, code, first, room):
    block = 128
    panels = value.shape[1] // block
    out = []
    for j in range(room):
        total = None
        for p in range(panels):
            at = slice(p * block, (p + 1) * block)
            part = jnp.where(code[:, at] == first + j, value[:, at], 0.0)
            total = part if total is None else total + part
        out.append(total)
    return jnp.concatenate(out, axis=1)


def place(value, code, first, room):
    block = 128
    panels = code.shape[1] // block
    out = []
    for p in range(panels):
        at = slice(p * block, (p + 1) * block)
        total = jnp.zeros((code.shape[0], block), F32)
        for j in range(room):
            total = total + jnp.where(code[:, at] == first + j, value[:, j * block : (j + 1) * block], 0.0)
        out.append(total)
    return jnp.concatenate(out, axis=1)


def solve(value, high_ref, low_ref, form):
    rows, block = value.shape[0], high_ref.shape[1]
    out = []
    for p in range(high_ref.shape[0]):
        panel = value[:, p * block : (p + 1) * block]
        top = panel.astype(BF16).astype(F32)
        both = jnp.concatenate([top, panel - top], axis=0).astype(BF16)
        product = matmul(both, high_ref[p], form) + matmul(both, low_ref[p], form)
        out.append(product[:rows] + product[rows:])
    return jnp.concatenate(out, axis=1)


def in_level(code, level, panels):
    return (code >= level * panels) & (code < (level + 1) * panels)


def start_kernel(
    order_hbm, load_hbm, inverse_hbm, front_hbm,
    row_code_ref, col_code_ref, high_ref, low_ref, mine_ref, y_ref, send_ref, front_ref, choice_ref,
    order_ref, load_ref, inverse_ref, sems,
):
    panels, block = high_ref.shape[0], high_ref.shape[1]
    vectors = load_ref.shape[0] // 2
    copies = [
        pltpu.make_async_copy(order_hbm, order_ref, sems.at[0]),
        pltpu.make_async_copy(load_hbm, load_ref, sems.at[1]),
        pltpu.make_async_copy(inverse_hbm, inverse_ref, sems.at[2]),
        pltpu.make_async_copy(front_hbm, front_ref, sems.at[3]),
    ]
    for copy in copies:
        copy.start()
    copies[0].wait()
    order = jnp.broadcast_to(order_ref[...], (2 * panels, order_ref.shape[1]))
    per_level = order.shape[1] // LEVELS
    panel = lax.broadcasted_iota(jnp.int32, order.shape, 0)
    of_rows = panel < panels
    place_in = jnp.where(of_rows, panel, panel - panels)
    names = jnp.where(of_rows, lax.axis_index(PLANE), lax.axis_index("z")) * panels + place_in
    counting = lax.broadcasted_iota(jnp.int32, order.shape, 1)
    ranks = jnp.sum(jnp.where(order == names, counting, 0), axis=1, keepdims=True)
    levels = jnp.zeros_like(ranks)
    for bound in range(1, LEVELS):
        levels = levels + jnp.where(ranks >= bound * per_level, 1, 0)
    levels = jnp.broadcast_to(levels, order.shape)
    codes = levels * panels
    for p in range(panels - 1):
        same = levels == jnp.where(of_rows, levels[p : p + 1], levels[panels + p : panels + p + 1])
        codes = codes + jnp.where(same & (place_in > p), 1, 0)
    spread_codes = [jnp.broadcast_to(codes[p : p + 1], (vectors, block)) for p in range(2 * panels)]
    row_code = jnp.concatenate(spread_codes[:panels], axis=1)
    row_code_ref[...] = row_code
    col_code_ref[...] = jnp.concatenate(spread_codes[panels:], axis=1)
    inside = order // panels == panel
    most = jnp.zeros((2 * panels, 1), jnp.int32)
    for level in range(LEVELS):
        of_level = inside & (counting >= level * per_level) & (counting < (level + 1) * per_level)
        most = jnp.maximum(most, jnp.sum(jnp.where(of_level, 1, 0), axis=1, keepdims=True))
    choice = jnp.zeros_like(most)
    for room in ROOM:
        choice = choice + jnp.where(most > room, 1, 0)
    choice_ref[0] = jnp.max(choice)
    copies[1].wait()
    load = jnp.where(lax.axis_index("k") == 0, load_ref[:vectors], load_ref[vectors:])
    mine_ref[...] = load
    copies[2].wait()
    high, low = split(inverse_ref[...])
    high_ref[...] = high
    low_ref[...] = low
    y = jnp.where(in_level(row_code, 0, panels), solve(load, high_ref, low_ref, "nt"), 0.0)
    y_ref[...] = y
    send_to_all(send_ref, y)
    copies[3].wait()


def update_kernel(level, room, front_ref, partner_ref, got_ref, row_code_ref, col_code_ref, *refs):
    first, last = level == 1, level == LEVELS - 1
    got = got_ref[lax.axis_index("z")]
    if not first:
        got = place(got.astype(F32), col_code_ref[...], (level - 1) * 8, room).astype(BF16)
    half = front_ref.shape[1]
    left, right = got[:, :half], got[:, half:]
    on_left = lax.axis_index("k") == 0
    out = matmul(jnp.where(on_left, left, right), front_ref[...], "nt") + matmul(
        jnp.where(on_left, right, left), partner_ref[...], "nt"
    )
    if not first:
        out = refs[0][...] + out
    if not last:
        refs[-2][...] = out
    send_to_all(refs[-1], pick(out, row_code_ref[...], level * 8, room))


def forward_step(level, room, got_ref, mine_ref, code, high_ref, low_ref):
    return solve(mine_ref[...] - place(sum_slots(got_ref), code, level * 8, room), high_ref, low_ref, "nt")


def forward_kernel(level, room, got_ref, mine_ref, row_code_ref, high_ref, low_ref, y_in_ref, y_ref, send_ref):
    code = row_code_ref[...]
    candidate = forward_step(level, room, got_ref, mine_ref, code, high_ref, low_ref)
    y_ref[...] = jnp.where(in_level(code, level, 8), candidate, y_in_ref[...])
    send_to_all(send_ref, pick(candidate, code, level * 8, room))


def back_product(x, front_ref, partner_ref):
    x = x.astype(BF16)
    own, other = matmul(x, front_ref[...], "nn"), matmul(x, partner_ref[...], "nn")
    first = lax.axis_index("k") == 0
    return jnp.concatenate([jnp.where(first, own, other), jnp.where(first, other, own)], axis=1)


def turn_kernel(
    room, front_ref, partner_ref, got_ref, mine_ref, row_code_ref, col_code_ref, high_ref, low_ref, y_in_ref,
    modes_hbm, y_ref, x_ref, pending_ref, send_ref, modes_ref, sem,
):
    modes_copy = pltpu.make_async_copy(modes_hbm, modes_ref, sem)
    modes_copy.start()
    code = row_code_ref[...]
    level = LEVELS - 1
    chosen = in_level(code, level, 8)
    candidate = forward_step(level, room, got_ref, mine_ref, code, high_ref, low_ref)
    y = jnp.where(chosen, candidate, y_in_ref[...])
    y_ref[...] = y
    x = jnp.where(chosen, solve(y, high_ref, low_ref, "nn"), 0.0)
    x_ref[...] = x
    out = back_product(x, front_ref, partner_ref)
    pending_ref[...] = out
    send_to_all(send_ref, pick(out, col_code_ref[...], (level - 1) * 8, room))
    modes_copy.wait()


def back_kernel(level, room, got_ref, col_code_ref, high_ref, low_ref, y_ref, send_ref):
    code = col_code_ref[...]
    here = place(sum_slots(got_ref), code, level * 8, room)
    send_to_all(send_ref, pick(solve(y_ref[...] - here, high_ref, low_ref, "nn"), code, level * 8, room))


def fresh_rows(level, room, got_ref, row_code_ref):
    got = got_ref[lax.axis_index(PLANE)].astype(F32)
    return place(got, row_code_ref[...], level * 8, room)


def back_update_kernel(
    level, room, front_ref, partner_ref, got_ref, row_code_ref, col_code_ref, x_in_ref, pending_in_ref, x_ref, *refs
):
    fresh = fresh_rows(level, room, got_ref, row_code_ref)
    x_ref[...] = x_in_ref[...] + fresh
    out = pending_in_ref[...] + back_product(fresh, front_ref, partner_ref)
    if level > 1:
        refs[0][...] = out
    send_to_all(refs[-1], pick(out, col_code_ref[...], (level - 1) * 8, room))


def last_pick_kernel(room, got_ref, row_code_ref, x_in_ref, x_ref):
    x_ref[...] = x_in_ref[...] + fresh_rows(0, room, got_ref, row_code_ref)


def coords_kernel(pair_ref, tie_ref, mass_ref, modes_ref, x_ref, static_ref, send_ref):
    x = jnp.concatenate([pair_ref[0], pair_ref[1]], axis=0)
    x_ref[...] = x
    static = tie_ref[...] * x
    static_ref[...] = static
    coords = matmul((mass_ref[...] * static).astype(BF16), modes_ref[...], "nt").astype(BF16)
    cores, half = 2, send_ref.shape[2]
    for slot in range(send_ref.shape[0]):
        part = slot % cores
        send_ref[slot] = coords[:, part * half : (part + 1) * half]


def relay_kernel(got_ref, send_ref):
    send_to_all(send_ref, sum_slots(got_ref))


def gathered_kernel(got_ref, out_ref):
    out_ref[...] = sum_slots(got_ref).astype(BF16)


def finish_kernel(static_ref, pair_ref, modes_ref, x_ref, whole_ref, out_ref):
    half = pair_ref.shape[2]
    correction = matmul(pair_ref[0], modes_ref[:half], "nn") + matmul(pair_ref[1], modes_ref[half:], "nn")
    whole_ref[...] = x_ref[...]
    out_ref[:, 0, :] = static_ref[...] - correction


def bound(body, *settings):
    def kernel(*refs):
        return body(*settings, *refs)

    return kernel


def on_device(front, diag_inverse, load, panel_order, tie, mass, modes):
    vectors = load.shape[0]
    rows, half = front.shape
    plane = lax.axis_size(PLANE)
    depth = lax.axis_size("z")
    cores = lax.axis_size("k")
    mode_rows = modes.reshape(modes.shape[0], -1)

    part = vectors // cores
    panels, block = diag_inverse.shape[0], diag_inverse.shape[1]
    flat = ((part, rows), F32)
    coded = ((part, rows), jnp.int32)
    inverse_part = (diag_inverse.shape, BF16)
    narrow = ((vectors, half), BF16)
    to_depth = ((depth, vectors, half), BF16)

    def exchange(value, axes):
        return lax.all_to_all(value, axes, 0, 0, tiled=True)

    def both_cores(value):
        return lax.all_gather(value, "k", axis=0)

    partner = lax.ppermute(front, "k", [(core, 1 - core) for core in range(cores)])
    row_code, col_code, high, low, mine, y, send, front, choice = call(
        start_kernel,
        [coded, coded, inverse_part, inverse_part, flat, flat, ((plane, part, rows), BF16),
         (front.shape, BF16), CHOICE],
        Far(panel_order[None, :]), Far(load), Far(diag_inverse), Far(front),
        scratch=[
            pltpu.VMEM((1, panel_order.shape[0]), jnp.int32),
            pltpu.VMEM(load.shape, F32),
            pltpu.VMEM(diag_inverse.shape, F32),
            pltpu.SemaphoreType.DMA((4,)),
        ],
    )

    got, choice = lax.optimization_barrier((exchange(send, PLANE), choice))

    def solve_levels(room, front, partner, got, row_code, col_code, high, low, mine, y, mode_rows):
        mode_shape = mode_rows.shape
        slots = ((plane, part, room * block), BF16)
        deep = ((depth, part, room * block), BF16)
        pending = ()
        for level in range(1, LEVELS):
            last = level == LEVELS - 1
            *pending, send = call(
                bound(update_kernel, level, room),
                [deep] if last else [flat, deep],
                front, partner, got, row_code, col_code, *pending,
            )
            got = exchange(send, "z")
            if not last:
                y, send = call(
                    bound(forward_kernel, level, room), [flat, slots], got, mine, row_code, high, low, y
                )
                got = exchange(send, PLANE)
        y, x, pending, send, mode_rows = call(
            bound(turn_kernel, room), [flat, flat, flat, slots, (mode_shape, BF16)],
            front, partner, got, mine, row_code, col_code, high, low, y, Far(mode_rows),
            scratch=[pltpu.SemaphoreType.DMA(())],
        )
        for level in reversed(range(LEVELS - 1)):
            (send,) = call(
                bound(back_kernel, level, room), [deep], exchange(send, PLANE), col_code, high, low, y
            )
            got = exchange(send, "z")
            if level > 0:
                x, *rest, send = call(
                    bound(back_update_kernel, level, room),
                    [flat, flat, slots] if level > 1 else [flat, slots],
                    front, partner, got, row_code, col_code, x, pending,
                )
                pending = rest[0] if rest else None
            else:
                (x,) = call(bound(last_pick_kernel, room), [flat], got, row_code, x)
        return x, mode_rows

    rooms = ROOM + (panels,)
    x, mode_rows = lax.switch(
        choice[0],
        [bound(solve_levels, room) for room in rooms],
        front, partner, got, row_code, col_code, high, low, mine, y, mode_rows,
    )

    whole, static, send = call(
        coords_kernel,
        [((vectors, rows), F32), ((vectors, rows), F32), ((plane * cores, vectors, half), BF16)],
        both_cores(x), tie, mass, mode_rows,
    )
    (send,) = call(relay_kernel, [to_depth], exchange(send, PLANE + ("k",)))
    (coords,) = call(gathered_kernel, [narrow], exchange(send, "z"))
    return tuple(
        call(
            finish_kernel,
            [jax.ShapeDtypeStruct((vectors, rows), F32), jax.ShapeDtypeStruct((vectors, 1, rows), F32)],
            static, both_cores(coords), mode_rows, whole,
        )
    )


def solution(mesh):
    grid = Mesh(mesh.devices.reshape(4, 4, 16, 2), PLANE + ("z", "k"))
    row, col = PLANE, ("z", "k")
    in_specs = (
        P(row, col),
        P(row, None, None),
        P(None, row),
        P(),
        P(col, row),
        P(col, row),
        P(None, col, row),
    )
    out_specs = (P(None, row), P(None, col, row))
    return jax.shard_map(
        on_device, mesh=grid, in_specs=in_specs, out_specs=out_specs, check_vma=False
    )
```

```python
import jax
import jax.numpy as jnp
from jax import lax
from jax.experimental import pallas as pl
from jax.experimental.pallas import tpu as pltpu
from jax.sharding import Mesh, PartitionSpec as P

LEVELS = 4
ROOM = (4, 5, 6)
PLANE = ("x", "y")
F32, BF16 = jnp.float32, jnp.bfloat16


def matmul(a, b, form):
    dims = {"nn": (((1,), (0,)), ((), ())), "nt": (((1,), (1,)), ((), ()))}[form]
    return lax.dot_general(a, b, dims, preferred_element_type=F32)


def split(value):
    high = value.astype(BF16)
    return high, (value - high.astype(F32)).astype(BF16)


CHOICE = pltpu.SMEM((1,), jnp.int32)


class Far:
    def __init__(self, array):
        self.array = array


def call(body, outs, *args, scratch=()):
    vmem = pl.BlockSpec(memory_space=pltpu.VMEM)
    in_specs, given = [], []
    for arg in args:
        if isinstance(arg, Far):
            in_specs.append(pl.BlockSpec(memory_space=pltpu.HBM))
            given.append(pltpu.with_memory_space_constraint(arg.array, pltpu.HBM))
        else:
            in_specs.append(vmem)
            given.append(pltpu.with_memory_space_constraint(arg, pltpu.VMEM))
    return pl.pallas_call(
        body,
        out_shape=[pltpu.VMEM(*out) if isinstance(out, tuple) else out for out in outs],
        in_specs=in_specs,
        out_specs=[pl.BlockSpec(memory_space=pltpu.SMEM) if out is CHOICE else vmem for out in outs],
        scratch_shapes=list(scratch),
        compiler_params=pltpu.CompilerParams(vmem_limit_bytes=8 << 20),
    )(*given)


def send_to_all(out_ref, value):
    value = value.astype(BF16)
    for slot in range(out_ref.shape[0]):
        out_ref[slot] = value


def sum_slots(ref):
    total = ref[0].astype(F32)
    for slot in range(1, ref.shape[0]):
        total = total + ref[slot].astype(F32)
    return total


def pick(value, code, first, room):
    block = 128
    panels = value.shape[1] // block
    out = []
    for j in range(room):
        total = None
        for p in range(panels):
            at = slice(p * block, (p + 1) * block)
            part = jnp.where(code[:, at] == first + j, value[:, at], 0.0)
            total = part if total is None else total + part
        out.append(total)
    return jnp.concatenate(out, axis=1)


def place(value, code, first, room):
    block = 128
    panels = code.shape[1] // block
    out = []
    for p in range(panels):
        at = slice(p * block, (p + 1) * block)
        total = jnp.zeros((code.shape[0], block), F32)
        for j in range(room):
            total = total + jnp.where(code[:, at] == first + j, value[:, j * block : (j + 1) * block], 0.0)
        out.append(total)
    return jnp.concatenate(out, axis=1)


def solve(value, high_ref, low_ref, form):
    rows, block = value.shape[0], high_ref.shape[1]
    out = []
    for p in range(high_ref.shape[0]):
        panel = value[:, p * block : (p + 1) * block]
        top = panel.astype(BF16).astype(F32)
        both = jnp.concatenate([top, panel - top], axis=0).astype(BF16)
        product = matmul(both, high_ref[p], form) + matmul(both, low_ref[p], form)
        out.append(product[:rows] + product[rows:])
    return jnp.concatenate(out, axis=1)


def in_level(code, level, panels):
    return (code >= level * panels) & (code < (level + 1) * panels)


def start_kernel(
    order_hbm, load_hbm, inverse_hbm, front_hbm,
    row_code_ref, col_code_ref, high_ref, low_ref, mine_ref, y_ref, send_ref, front_ref, choice_ref,
    order_ref, load_ref, inverse_ref, sems,
):
    panels, block = high_ref.shape[0], high_ref.shape[1]
    vectors = load_ref.shape[0] // 2
    copies = [
        pltpu.make_async_copy(order_hbm, order_ref, sems.at[0]),
        pltpu.make_async_copy(load_hbm, load_ref, sems.at[1]),
        pltpu.make_async_copy(inverse_hbm, inverse_ref, sems.at[2]),
        pltpu.make_async_copy(front_hbm, front_ref, sems.at[3]),
    ]
    for copy in copies:
        copy.start()
    copies[0].wait()
    order = jnp.broadcast_to(order_ref[...], (2 * panels, order_ref.shape[1]))
    per_level = order.shape[1] // LEVELS
    panel = lax.broadcasted_iota(jnp.int32, order.shape, 0)
    of_rows = panel < panels
    place_in = jnp.where(of_rows, panel, panel - panels)
    names = jnp.where(of_rows, lax.axis_index(PLANE), lax.axis_index("z")) * panels + place_in
    counting = lax.broadcasted_iota(jnp.int32, order.shape, 1)
    ranks = jnp.sum(jnp.where(order == names, counting, 0), axis=1, keepdims=True)
    levels = jnp.zeros_like(ranks)
    for bound in range(1, LEVELS):
        levels = levels + jnp.where(ranks >= bound * per_level, 1, 0)
    levels = jnp.broadcast_to(levels, order.shape)
    codes = levels * panels
    for p in range(panels - 1):
        same = levels == jnp.where(of_rows, levels[p : p + 1], levels[panels + p : panels + p + 1])
        codes = codes + jnp.where(same & (place_in > p), 1, 0)
    spread_codes = [jnp.broadcast_to(codes[p : p + 1], (vectors, block)) for p in range(2 * panels)]
    row_code = jnp.concatenate(spread_codes[:panels], axis=1)
    row_code_ref[...] = row_code
    col_code_ref[...] = jnp.concatenate(spread_codes[panels:], axis=1)
    inside = order // panels == panel
    most = jnp.zeros((2 * panels, 1), jnp.int32)
    for level in range(LEVELS):
        of_level = inside & (counting >= level * per_level) & (counting < (level + 1) * per_level)
        most = jnp.maximum(most, jnp.sum(jnp.where(of_level, 1, 0), axis=1, keepdims=True))
    choice = jnp.zeros_like(most)
    for room in ROOM:
        choice = choice + jnp.where(most > room, 1, 0)
    choice_ref[0] = jnp.max(choice)
    copies[1].wait()
    load = jnp.where(lax.axis_index("k") == 0, load_ref[:vectors], load_ref[vectors:])
    mine_ref[...] = load
    copies[2].wait()
    high, low = split(inverse_ref[...])
    high_ref[...] = high
    low_ref[...] = low
    y = jnp.where(in_level(row_code, 0, panels), solve(load, high_ref, low_ref, "nt"), 0.0)
    y_ref[...] = y
    send_to_all(send_ref, y)
    copies[3].wait()


def update_kernel(level, room, front_ref, partner_ref, got_ref, row_code_ref, col_code_ref, *refs):
    first, last = level == 1, level == LEVELS - 1
    got = got_ref[lax.axis_index("z")]
    if not first:
        got = place(got.astype(F32), col_code_ref[...], (level - 1) * 8, room).astype(BF16)
    half = front_ref.shape[1]
    left, right = got[:, :half], got[:, half:]
    on_left = lax.axis_index("k") == 0
    out = matmul(jnp.where(on_left, left, right), front_ref[...], "nt") + matmul(
        jnp.where(on_left, right, left), partner_ref[...], "nt"
    )
    if not first:
        out = refs[0][...] + out
    if not last:
        refs[-2][...] = out
    send_to_all(refs[-1], pick(out, row_code_ref[...], level * 8, room))


def forward_step(level, room, got_ref, mine_ref, code, high_ref, low_ref):
    return solve(mine_ref[...] - place(sum_slots(got_ref), code, level * 8, room), high_ref, low_ref, "nt")


def forward_kernel(level, room, got_ref, mine_ref, row_code_ref, high_ref, low_ref, y_in_ref, y_ref, send_ref):
    code = row_code_ref[...]
    candidate = forward_step(level, room, got_ref, mine_ref, code, high_ref, low_ref)
    y_ref[...] = jnp.where(in_level(code, level, 8), candidate, y_in_ref[...])
    send_to_all(send_ref, pick(candidate, code, level * 8, room))


def back_product(x, front_ref, partner_ref):
    x = x.astype(BF16)
    own, other = matmul(x, front_ref[...], "nn"), matmul(x, partner_ref[...], "nn")
    first = lax.axis_index("k") == 0
    return jnp.concatenate([jnp.where(first, own, other), jnp.where(first, other, own)], axis=1)


def turn_kernel(
    room, front_ref, partner_ref, got_ref, mine_ref, row_code_ref, col_code_ref, high_ref, low_ref, y_in_ref,
    modes_hbm, y_ref, x_ref, pending_ref, send_ref, modes_ref, sem,
):
    size = modes_ref.shape[0] // sem.shape[0]
    copies = [
        pltpu.make_async_copy(modes_hbm.at[pl.ds(i * size, size)], modes_ref.at[pl.ds(i * size, size)], sem.at[i])
        for i in range(sem.shape[0])
    ]
    for copy in copies:
        copy.start()
    code = row_code_ref[...]
    level = LEVELS - 1
    chosen = in_level(code, level, 8)
    candidate = forward_step(level, room, got_ref, mine_ref, code, high_ref, low_ref)
    y = jnp.where(chosen, candidate, y_in_ref[...])
    y_ref[...] = y
    x = jnp.where(chosen, solve(y, high_ref, low_ref, "nn"), 0.0)
    x_ref[...] = x
    out = back_product(x, front_ref, partner_ref)
    pending_ref[...] = out
    send_to_all(send_ref, pick(out, col_code_ref[...], (level - 1) * 8, room))
    for copy in copies:
        copy.wait()


def back_kernel(level, room, got_ref, col_code_ref, high_ref, low_ref, y_ref, send_ref):
    code = col_code_ref[...]
    here = place(sum_slots(got_ref), code, level * 8, room)
    send_to_all(send_ref, pick(solve(y_ref[...] - here, high_ref, low_ref, "nn"), code, level * 8, room))


def fresh_rows(level, room, got_ref, row_code_ref):
    got = got_ref[lax.axis_index(PLANE)].astype(F32)
    return place(got, row_code_ref[...], level * 8, room)


def back_update_kernel(
    level, room, front_ref, partner_ref, got_ref, row_code_ref, col_code_ref, x_in_ref, pending_in_ref, x_ref, *refs
):
    fresh = fresh_rows(level, room, got_ref, row_code_ref)
    x_ref[...] = x_in_ref[...] + fresh
    out = pending_in_ref[...] + back_product(fresh, front_ref, partner_ref)
    if level > 1:
        refs[0][...] = out
    send_to_all(refs[-1], pick(out, col_code_ref[...], (level - 1) * 8, room))


def last_pick_kernel(room, got_ref, row_code_ref, x_in_ref, x_ref):
    x_ref[...] = x_in_ref[...] + fresh_rows(0, room, got_ref, row_code_ref)


def coords_kernel(pair_ref, tie_ref, mass_ref, modes_ref, x_ref, static_ref, send_ref):
    x = jnp.concatenate([pair_ref[0], pair_ref[1]], axis=0)
    x_ref[...] = x
    static = tie_ref[...] * x
    static_ref[...] = static
    coords = matmul((mass_ref[...] * static).astype(BF16), modes_ref[...], "nt").astype(BF16)
    cores, half = 2, send_ref.shape[2]
    for slot in range(send_ref.shape[0]):
        part = slot % cores
        send_ref[slot] = coords[:, part * half : (part + 1) * half]


def relay_kernel(got_ref, send_ref):
    send_to_all(send_ref, sum_slots(got_ref))


def gathered_kernel(got_ref, out_ref):
    out_ref[...] = sum_slots(got_ref).astype(BF16)


def finish_kernel(static_ref, pair_ref, modes_ref, x_ref, whole_ref, out_ref):
    half = pair_ref.shape[2]
    correction = matmul(pair_ref[0], modes_ref[:half], "nn") + matmul(pair_ref[1], modes_ref[half:], "nn")
    whole_ref[...] = x_ref[...]
    out_ref[:, 0, :] = static_ref[...] - correction


def bound(body, *settings):
    def kernel(*refs):
        return body(*settings, *refs)

    return kernel


def on_device(front, diag_inverse, load, panel_order, tie, mass, modes):
    vectors = load.shape[0]
    rows, half = front.shape
    plane = lax.axis_size(PLANE)
    depth = lax.axis_size("z")
    cores = lax.axis_size("k")
    mode_rows = modes.reshape(modes.shape[0], -1)

    part = vectors // cores
    panels, block = diag_inverse.shape[0], diag_inverse.shape[1]
    flat = ((part, rows), F32)
    coded = ((part, rows), jnp.int32)
    inverse_part = (diag_inverse.shape, BF16)
    narrow = ((vectors, half), BF16)
    to_depth = ((depth, vectors, half), BF16)

    def exchange(value, axes):
        return lax.all_to_all(value, axes, 0, 0, tiled=True)

    def both_cores(value):
        return lax.all_gather(value, "k", axis=0)

    partner = lax.ppermute(front, "k", [(core, 1 - core) for core in range(cores)])
    row_code, col_code, high, low, mine, y, send, front, choice = call(
        start_kernel,
        [coded, coded, inverse_part, inverse_part, flat, flat, ((plane, part, rows), BF16),
         (front.shape, BF16), CHOICE],
        Far(panel_order[None, :]), Far(load), Far(diag_inverse), Far(front),
        scratch=[
            pltpu.VMEM((1, panel_order.shape[0]), jnp.int32),
            pltpu.VMEM(load.shape, F32),
            pltpu.VMEM(diag_inverse.shape, F32),
            pltpu.SemaphoreType.DMA((4,)),
        ],
    )

    got, choice = lax.optimization_barrier((exchange(send, PLANE), choice))

    def solve_levels(room, front, partner, got, row_code, col_code, high, low, mine, y, mode_rows):
        mode_shape = mode_rows.shape
        slots = ((plane, part, room * block), BF16)
        deep = ((depth, part, room * block), BF16)
        pending = ()
        for level in range(1, LEVELS):
            last = level == LEVELS - 1
            *pending, send = call(
                bound(update_kernel, level, room),
                [deep] if last else [flat, deep],
                front, partner, got, row_code, col_code, *pending,
            )
            got = exchange(send, "z")
            if not last:
                y, send = call(
                    bound(forward_kernel, level, room), [flat, slots], got, mine, row_code, high, low, y
                )
                got = exchange(send, PLANE)
        y, x, pending, send, mode_rows = call(
            bound(turn_kernel, room), [flat, flat, flat, slots, (mode_shape, BF16)],
            front, partner, got, mine, row_code, col_code, high, low, y, Far(mode_rows),
            scratch=[pltpu.SemaphoreType.DMA((4,))],
        )
        for level in reversed(range(LEVELS - 1)):
            (send,) = call(
                bound(back_kernel, level, room), [deep], exchange(send, PLANE), col_code, high, low, y
            )
            got = exchange(send, "z")
            if level > 0:
                x, *rest, send = call(
                    bound(back_update_kernel, level, room),
                    [flat, flat, slots] if level > 1 else [flat, slots],
                    front, partner, got, row_code, col_code, x, pending,
                )
                pending = rest[0] if rest else None
            else:
                (x,) = call(bound(last_pick_kernel, room), [flat], got, row_code, x)
        return x, mode_rows

    rooms = ROOM + (panels,)
    x, mode_rows = lax.switch(
        choice[0],
        [bound(solve_levels, room) for room in rooms],
        front, partner, got, row_code, col_code, high, low, mine, y, mode_rows,
    )

    whole, static, send = call(
        coords_kernel,
        [((vectors, rows), F32), ((vectors, rows), F32), ((plane * cores, vectors, half), BF16)],
        both_cores(x), tie, mass, mode_rows,
    )
    (send,) = call(relay_kernel, [to_depth], exchange(send, PLANE + ("k",)))
    (coords,) = call(gathered_kernel, [narrow], exchange(send, "z"))
    return tuple(
        call(
            finish_kernel,
            [jax.ShapeDtypeStruct((vectors, rows), F32), jax.ShapeDtypeStruct((vectors, 1, rows), F32)],
            static, both_cores(coords), mode_rows, whole,
        )
    )


def solution(mesh):
    grid = Mesh(mesh.devices.reshape(4, 4, 16, 2), PLANE + ("z", "k"))
    row, col = PLANE, ("z", "k")
    in_specs = (
        P(row, col),
        P(row, None, None),
        P(None, row),
        P(),
        P(col, row),
        P(col, row),
        P(None, col, row),
    )
    out_specs = (P(None, row), P(None, col, row))
    return jax.shard_map(
        on_device, mesh=grid, in_specs=in_specs, out_specs=out_specs, check_vma=False
    )
```
